32 devices in a mesh: gx: 2 (over core), gy: 4 (over y, x), gz: 4 (over z).
Axes of the slice: x: 2, y: 2, z: 4, core: 2. Of those that a mesh axis runs over, the one named last changes fastest.
Arguments:
- student: bfloat16 [1024, 1024], P('gx', 'gz'), may hold values from -12 to 12
- teacher: bfloat16 [8192, 1024], P('gy', 'gz'), may hold values from -6 to 6
- block_ids: int32 [8, 32], P('gx'), may hold values from 0 to 63, as said below
- block_valid: int32 [8, 32], P('gx'), may hold values from 0 to 1
Outputs:
- row_potential: float32 [1024], P('gx')
- column_potential: float32 [8192], P('gy')
The draws below stay inside these ranges and needn't reach their ends.
Inputs may be any that keep to these rules, and one draw needn't show every extreme that they name: `block_ids`: within each row block the valid slots name distinct column blocks, and at most 8 of them lie in one aligned group of 16 column blocks; in every draw some row block has exactly 8 valid slots in one group.
All inputs are finite; a program needn't handle non-finite values.
Results may differ from the reference program's by a relative error of at most 0.0003.
Values sent between devices are 32-bit elements; how exact they have to be, the bound alone decides.
A program may use at most 64 MiB of HBM per device.

```python
import math
import jax
import jax.numpy as jnp
from jax import lax

F = 1024
TILE = 128
SLOTS = 32
LOCAL_MOST = 8
ITERS = 5
CB_DEV = 16
RBLOCKS = 8
CBLOCKS = 64


def mask_tables(key):
    base_key = jax.random.fold_in(key, 4411)
    range_count = CBLOCKS // CB_DEV
    width_all = range_count * LOCAL_MOST
    key_pick = jax.random.fold_in(base_key, 1)
    key_bias = jax.random.fold_in(base_key, 2)
    key_favor = jax.random.fold_in(base_key, 3)
    key_jitter = jax.random.fold_in(base_key, 4)
    key_count = jax.random.fold_in(base_key, 5)
    key_count_two = jax.random.fold_in(base_key, 6)
    key_forced = jax.random.fold_in(base_key, 7)
    key_shuffle = jax.random.fold_in(base_key, 8)
    pick_scores = jax.random.randint(key_pick, (RBLOCKS, range_count, CB_DEV), 0, 1 << 20) * CB_DEV + jnp.arange(CB_DEV, dtype=jnp.int32)[None, None, :]
    picked = jnp.argsort(pick_scores, axis=2)[:, :, :LOCAL_MOST].astype(jnp.int32)
    candidates = (picked + (jnp.arange(range_count, dtype=jnp.int32) * CB_DEV)[None, :, None]).reshape(RBLOCKS, width_all)
    range_bias = jax.random.randint(key_bias, (RBLOCKS, range_count), 0, 3)
    favored = jax.random.randint(key_favor, (RBLOCKS,), 0, range_count)
    range_bias = jnp.where(jnp.arange(range_count, dtype=jnp.int32)[None, :] == favored[:, None], 3, range_bias)
    jitter = jax.random.randint(key_jitter, (RBLOCKS, range_count, LOCAL_MOST), 0, 1 << 16)
    priority = range_bias[:, :, None] * (1 << 26) + jitter * 256
    priority = priority.reshape(RBLOCKS, width_all) + jnp.arange(width_all, dtype=jnp.int32)[None, :]
    ranking = jnp.argsort(-priority, axis=1)[:, :SLOTS].astype(jnp.int32)
    chosen = jnp.take_along_axis(candidates, ranking, axis=1)
    counts = SLOTS - 1 - jax.random.randint(key_count, (RBLOCKS,), 0, SLOTS) * jax.random.randint(key_count_two, (RBLOCKS,), 0, SLOTS) // SLOTS
    counts = jnp.maximum(counts, 1)
    forced_row = jax.random.randint(key_forced, (), 0, RBLOCKS)
    counts = jnp.where(jnp.arange(RBLOCKS, dtype=jnp.int32) == forced_row, SLOTS, counts)
    valid_sorted = (jnp.arange(SLOTS, dtype=jnp.int32)[None, :] < counts[:, None]).astype(jnp.int32)
    shuffle_scores = jax.random.randint(key_shuffle, (RBLOCKS, SLOTS), 0, 1 << 20) * SLOTS + jnp.arange(SLOTS, dtype=jnp.int32)[None, :]
    shuffle_order = jnp.argsort(shuffle_scores, axis=1).astype(jnp.int32)
    block_ids = jnp.take_along_axis(chosen, shuffle_order, axis=1).astype(jnp.int32)
    block_valid = jnp.take_along_axis(valid_sorted, shuffle_order, axis=1).astype(jnp.int32)
    return (block_ids, block_valid)


def teacher_table(key):
    base_key = jax.random.fold_in(key, 5303)
    values = jnp.clip(jax.random.normal(base_key, (CBLOCKS * TILE, F), jnp.float32), -6.0, 6.0)
    return values


def draw_block_ids(key, part):
    return mask_tables(key)[0]


def draw_block_valid(key, part):
    return mask_tables(key)[1]


def draw_teacher(key, part):
    return teacher_table(key).astype(jnp.bfloat16)


def draw_student(key, part):
    base_key = jax.random.fold_in(key, 5404)
    values = jnp.clip(jax.random.normal(base_key, (RBLOCKS * TILE, F), jnp.float32), -6.0, 6.0)
    return jnp.clip(values, -12.0, 12.0).astype(jnp.bfloat16)


def setup_inputs(seed: int = 0) -> dict:
    arg_keys = jax.random.split(jax.random.key(seed), 5)
    return {
        "student": draw_student(jax.random.fold_in(arg_keys[4], 71), 0),
        "teacher": draw_teacher(jax.random.fold_in(arg_keys[4], 71), 0),
        "block_ids": draw_block_ids(jax.random.fold_in(arg_keys[4], 71), 0),
        "block_valid": draw_block_valid(jax.random.fold_in(arg_keys[4], 71), 0),
    }


SOFTNESS = 0.1

def soft_bound(highest, totals):
    return -SOFTNESS * (highest + jnp.log(totals + jnp.exp(-highest)))

def reference(student, teacher, block_ids, block_valid):
    cost_scale = -1.0 / math.sqrt(F)
    student_blocks = student.astype(jnp.float32).reshape(RBLOCKS, TILE, F)
    teacher_blocks = teacher.astype(jnp.float32).reshape(CBLOCKS, TILE, F)
    slot_live = block_valid > 0

    def tile_costs(inputs):
        slot_ids, rows_here = inputs
        chosen = teacher_blocks[slot_ids]
        return jnp.einsum('scf,if->sci', chosen, rows_here) * cost_scale
    costs = lax.map(tile_costs, (block_ids, student_blocks))
    column_values = jnp.zeros((CBLOCKS, TILE), jnp.float32)
    row_values = jnp.zeros((RBLOCKS, TILE), jnp.float32)
    for sweep in range(ITERS):

        def row_update(inputs):
            tile_cost, slot_ids, live_here = inputs
            scores = (column_values[slot_ids][:, :, None] - tile_cost) / SOFTNESS
            live_mask = live_here[:, None, None]
            highest = jnp.maximum(lax.optimization_barrier(jnp.max(jnp.where(live_mask, scores, -1e+30), axis=(0, 1))), 0.0)
            totals = lax.optimization_barrier(jnp.sum(jnp.where(live_mask, jnp.exp(scores - highest[None, None, :]), 0.0), axis=(0, 1)))
            return soft_bound(highest, totals)
        row_values = lax.map(row_update, (costs, block_ids, slot_live))

        def column_step(state_pair, inputs):
            highest, totals = state_pair
            tile_cost, slot_ids, live_here, row_here = inputs
            scores = (row_here[None, None, :] - tile_cost) / SOFTNESS
            tile_peak = jnp.where(live_here[:, None], lax.optimization_barrier(jnp.max(scores, axis=2)), 0.0)
            raised = highest.at[slot_ids].max(tile_peak)
            tile_sum = jnp.where(live_here[:, None], lax.optimization_barrier(jnp.sum(jnp.exp(scores - raised[slot_ids][:, :, None]), axis=2)), 0.0)
            totals = totals * jnp.exp(highest - raised) + jnp.zeros_like(totals).at[slot_ids].add(tile_sum)
            return ((raised, totals), None)
        start_pair = (jnp.zeros((CBLOCKS, TILE), jnp.float32), jnp.zeros((CBLOCKS, TILE), jnp.float32))
        final_pair, unused = lax.scan(column_step, start_pair, (costs, block_ids, slot_live, row_values))
        column_values = soft_bound(final_pair[0], final_pair[1])
    return (row_values.reshape(-1), column_values.reshape(-1))
```

```python
import functools
import math

import jax
import jax.numpy as jnp
from jax import lax
from jax.experimental import pallas as pl
from jax.experimental.pallas import tpu as pltpu
from jax.sharding import PartitionSpec as P

F = 1024
TILE = 128
ITERS = 5
SOFTNESS = 0.1
MESH = pl.DeviceIdType.MESH


def spread(values):
    return [
        jnp.broadcast_to(values[k : k + 1], (TILE, TILE)).T for k in range(values.shape[0])
    ]


def kernel(
    sizes, student, teacher, ids, valid, row_out, col_out,
    stu_stage, stu_buf, tea_stage, tea_buf, kern,
    first_send, first_recv, row_send, row_recv, col_send, col_recv, fin_recv,
    stu_ss, stu_rs, tea_ss, tea_rs, row_ss, row_rs, col_ss, col_rs,
):
    gx, gy, gz, chunks = sizes
    ix, iy, iz = lax.axis_index("gx"), lax.axis_index("gy"), lax.axis_index("gz")
    rows = student.shape[0]
    cols = teacher.shape[0] // gz
    row_blocks, col_blocks = rows // TILE, cols // TILE
    quarter = rows // gy
    part = cols // gx
    piece = part // chunks

    def peer(dx=0, dy=0, dz=0):
        return {
            "gx": lax.rem(ix + dx, gx),
            "gy": lax.rem(iy + dy, gy),
            "gz": lax.rem(iz + dz, gz),
        }

    def send(src, dst, send_sem, recv_sem, target):
        copy = pltpu.make_async_remote_copy(
            src_ref=src, dst_ref=dst, send_sem=send_sem, recv_sem=recv_sem,
            device_id=target, device_id_type=MESH,
        )
        copy.start()
        return copy

    row_peers = [(a, b) for a in range(gy) for b in range(gz) if a or b]
    end_peers = [(a, b) for a in range(gx) for b in range(gz) if a or b]
    barrier = pltpu.get_barrier_semaphore()
    greeted = [peer(dy=a, dz=b) for a, b in row_peers]
    greeted += [peer(dx=a, dz=b) for a, b in end_peers if a]
    for target in greeted:
        pl.semaphore_signal(barrier, inc=1, device_id=target, device_id_type=MESH)

    my_quarter = pl.ds(pl.multiple_of(iy * quarter, 8), quarter)
    stu_stage[...] = student[my_quarter, :].astype(jnp.float32)
    for d in range(1, gz):
        first = lax.rem(iz + d, gz) * cols + ix * part
        tea_stage[d - 1] = teacher[pl.ds(pl.multiple_of(first, 8), part), :].astype(jnp.float32)
    pl.semaphore_wait(barrier, len(greeted))

    order = sorted(range(1, gz), key=lambda d: min(d, gz - d))
    copies = []
    stu_first = {}
    for d in order[::-1]:
        stu_first[d] = send(
            stu_stage, stu_buf.at[d - 1, my_quarter], stu_ss.at[d - 1, 0],
            stu_rs.at[d - 1, 0], peer(dz=d),
        )
    tea_first = {}
    for c in range(chunks):
        for d in order[::-1]:
            here = pl.ds(c * piece, piece)
            there = pl.ds(pl.multiple_of(ix * part + c * piece, 8), piece)
            tea_first[d, c] = send(
                tea_stage.at[d - 1, here], tea_buf.at[d - 1, there],
                tea_ss.at[d - 1, 0, c], tea_rs.at[d - 1, 0, c], peer(dz=d),
            )
    copies += list(stu_first.values()) + list(tea_first.values())

    def product(a, b):
        return lax.dot_general(
            a, b, (((1,), (1,)), ((), ())), preferred_element_type=jnp.float32
        )

    mine = teacher[pl.ds(pl.multiple_of(iz * cols, 8), cols), :]
    kern[...] = product(student[...], mine)

    stu_second, tea_second = {}, {}
    for d in order:
        stu_first[d].wait_recv()
        block = stu_buf.at[d - 1, my_quarter]
        for e in range(1, gy):
            stu_second[d, e] = send(
                block, block, stu_ss.at[d - 1, e], stu_rs.at[d - 1, e], peer(dy=e)
            )
    for c in range(chunks):
        for d in order:
            tea_first[d, c].wait_recv()
            there = pl.ds(pl.multiple_of(ix * part + c * piece, 8), piece)
            block = tea_buf.at[d - 1, there]
            for e in range(1, gx):
                tea_second[d, c, e] = send(
                    block, block, tea_ss.at[d - 1, e, c], tea_rs.at[d - 1, e, c], peer(dx=e)
                )
    copies += list(stu_second.values()) + list(tea_second.values())
    for d in order:
        for e in range(1, gy):
            stu_second[d, e].wait_recv()
        for c in range(chunks):
            for e in range(1, gx):
                tea_second[d, c, e].wait_recv()
        kern[...] += product(
            stu_buf[d - 1].astype(jnp.bfloat16), tea_buf[d - 1].astype(jnp.bfloat16)
        )

    scale = 1.0 / (math.sqrt(F) * SOFTNESS)
    first_block = (iy * gz + iz) * col_blocks
    live_slot = valid[...] > 0
    hits = [
        jnp.max(jnp.where(live_slot & (ids[...] == first_block + c), 1.0, 0.0), axis=1, keepdims=True)
        for c in range(col_blocks)
    ]

    def tile(r, c):
        return pl.ds(r * TILE, TILE), pl.ds(c * TILE, TILE)

    peaks, sums = [], []
    for r in range(row_blocks):
        on = [jnp.broadcast_to(hits[c][r : r + 1], (TILE, TILE)) > 0 for c in range(col_blocks)]
        x = [kern[tile(r, c)] * scale for c in range(col_blocks)]
        top = functools.reduce(
            jnp.maximum, [jnp.where(on[c], x[c], 0.0) for c in range(col_blocks)]
        )
        peak = jnp.maximum(jnp.max(top.T, axis=0, keepdims=True), 0.0)
        base = spread(peak)[0]
        total = jnp.zeros((TILE, TILE), jnp.float32)
        for c in range(col_blocks):
            value = jnp.where(on[c], jnp.exp(jnp.minimum(x[c] - base, 0.0)), 0.0)
            kern[tile(r, c)] = value
            total += value
        peaks.append(peak)
        sums.append(jnp.sum(total.T, axis=0, keepdims=True))
    peak = jnp.concatenate(peaks, axis=0)
    total = jnp.concatenate(sums, axis=0)

    def exchange(src, dst, send_sem, recv_sem, targets):
        for k, target in enumerate(targets):
            send(src, dst.at[k], send_sem, recv_sem, target)
        pltpu.make_async_copy(dst, dst, recv_sem).wait()

    def sent(dst, send_sem):
        pltpu.make_async_copy(dst, dst, send_sem).wait()

    row_targets = [peer(dy=a, dz=b) for a, b in row_peers]
    col_targets = [peer(dx=a) for a in range(1, gx)]
    end_targets = [peer(dx=a, dz=b) for a, b in end_peers]

    first_send[0] = peak
    first_send[1] = total
    exchange(first_send, first_recv, row_ss.at[0], row_rs.at[0], row_targets)
    highest = functools.reduce(
        jnp.maximum, [first_recv[k, 0] for k in range(len(row_peers))], peak
    )
    totals = total * jnp.exp(peak - highest)
    for k in range(len(row_peers)):
        totals += first_recv[k, 1] * jnp.exp(first_recv[k, 0] - highest)
    level = highest + jnp.log(totals + jnp.exp(-highest))
    share = jnp.exp(peak - level)
    rest = jnp.exp(-level)
    row_total = None

    for t in range(ITERS):
        if t > 0:
            weights = 1.0 / (1.0 + col_total)
            parts = []
            for r in range(row_blocks):
                total = jnp.zeros((TILE, TILE), jnp.float32)
                for c in range(col_blocks):
                    total += kern[tile(r, c)] * weights[c : c + 1]
                parts.append(jnp.sum(total.T, axis=0, keepdims=True))
            own = jnp.concatenate(parts, axis=0) * share
            row_send[t - 1] = own
            exchange(
                row_send.at[t - 1], row_recv.at[t - 1], row_ss.at[t], row_rs.at[t], row_targets
            )
            row_total = rest + own
            for k in range(len(row_peers)):
                row_total += row_recv[t - 1, k]
            factors = spread(share / row_total)
        else:
            factors = spread(share)
        parts = []
        for c in range(col_blocks):
            total = jnp.zeros((TILE, TILE), jnp.float32)
            for r in range(row_blocks):
                total += kern[tile(r, c)] * factors[r]
            parts.append(jnp.sum(total, axis=0, keepdims=True))
        own = jnp.concatenate(parts, axis=0)
        col_send[t] = own
        if t < ITERS - 1:
            exchange(col_send.at[t], col_recv.at[t], col_ss.at[t], col_rs.at[t], col_targets)
            col_total = own
            for k in range(gx - 1):
                col_total += col_recv[t, k]
        else:
            exchange(col_send.at[t], fin_recv, col_ss.at[t], col_rs.at[t], end_targets)
            for b in range(gz):
                col_total = own if b == 0 else jnp.zeros_like(own)
                for k, (_, db) in enumerate(end_peers):
                    if db == b:
                        col_total += fin_recv[k]
                col_out[lax.rem(iz + gz - b, gz)] = -SOFTNESS * jnp.log(1.0 + col_total)
    row_out[...] = -SOFTNESS * (level + jnp.log(row_total))

    for copy in copies:
        copy.wait_send()
    sent(first_recv, row_ss.at[0])
    for t in range(1, ITERS):
        sent(row_recv.at[t - 1], row_ss.at[t])
        sent(col_recv.at[t - 1], col_ss.at[t - 1])
    sent(fin_recv, col_ss.at[ITERS - 1])


def solution(mesh):
    gx, gy, gz = (mesh.shape[axis] for axis in ("gx", "gy", "gz"))

    def on_device(student, teacher, block_ids, block_valid):
        rows, width = student.shape
        cols = teacher.shape[0] // gz
        row_blocks, col_blocks = rows // TILE, cols // TILE
        part = cols // gx
        chunks = max(1, min(4, part // 64))
        row_peers, end_peers = gy * gz - 1, gx * gz - 1
        f32 = jnp.float32
        dma = pltpu.SemaphoreType.DMA
        row, col = pl.pallas_call(
            functools.partial(kernel, (gx, gy, gz, chunks)),
            out_shape=(
                jax.ShapeDtypeStruct((row_blocks, TILE), f32),
                jax.ShapeDtypeStruct((gz, col_blocks, TILE), f32),
            ),
            in_specs=[pl.BlockSpec(memory_space=pltpu.VMEM)] * 4,
            out_specs=(pl.BlockSpec(memory_space=pltpu.VMEM),) * 2,
            scratch_shapes=[
                pltpu.VMEM((rows // gy, width), f32),
                pltpu.VMEM((gz - 1, rows, width), f32),
                pltpu.VMEM((gz - 1, part, width), f32),
                pltpu.VMEM((gz - 1, cols, width), f32),
                pltpu.VMEM((rows, cols), f32),
                pltpu.VMEM((2, row_blocks, TILE), f32),
                pltpu.VMEM((row_peers, 2, row_blocks, TILE), f32),
                pltpu.VMEM((ITERS - 1, row_blocks, TILE), f32),
                pltpu.VMEM((ITERS - 1, row_peers, row_blocks, TILE), f32),
                pltpu.VMEM((ITERS, col_blocks, TILE), f32),
                pltpu.VMEM((ITERS - 1, gx - 1, col_blocks, TILE), f32),
                pltpu.VMEM((end_peers, col_blocks, TILE), f32),
                dma((gz - 1, gy)),
                dma((gz - 1, gy)),
                dma((gz - 1, gx, chunks)),
                dma((gz - 1, gx, chunks)),
                dma((ITERS,)),
                dma((ITERS,)),
                dma((ITERS,)),
                dma((ITERS,)),
            ],
            compiler_params=pltpu.CompilerParams(collective_id=0, has_side_effects=True),
        )(student, teacher, block_ids, block_valid)
        return row.reshape(-1), col.reshape(-1)

    placed = (P("gx", "gz"), P("gy", "gz"), P("gx", None), P("gx", None))
    return jax.shard_map(
        on_device, mesh=mesh, in_specs=placed, out_specs=(P("gx"), P("gy")), check_vma=False
    )
```

```python
import functools
import math

import jax
import jax.numpy as jnp
from jax import lax
from jax.experimental import pallas as pl
from jax.experimental.pallas import tpu as pltpu
from jax.sharding import PartitionSpec as P

F = 1024
TILE = 128
ITERS = 5
SOFTNESS = 0.1
MESH = pl.DeviceIdType.MESH


def spread(values):
    return [
        jnp.broadcast_to(values[k : k + 1], (TILE, TILE)).T for k in range(values.shape[0])
    ]


def kernel(
    sizes, student, teacher, ids, valid, row_out, col_out,
    stu_stage, stu_buf, tea_stage, tea_buf, kern,
    first_send, first_recv, row_send, row_recv, col_send, col_recv, fin_recv,
    stu_ss, stu_rs, tea_ss, tea_rs, row_ss, row_rs, col_ss, col_rs,
):
    gx, gy, gz, chunks = sizes
    ix, iy, iz = lax.axis_index("gx"), lax.axis_index("gy"), lax.axis_index("gz")
    rows = student.shape[0]
    cols = teacher.shape[0] // gz
    row_blocks, col_blocks = rows // TILE, cols // TILE
    quarter = rows // gy
    part = cols // gx
    piece = part // chunks

    def peer(dx=0, dy=0, dz=0):
        return {
            "gx": lax.rem(ix + dx, gx),
            "gy": lax.rem(iy + dy, gy),
            "gz": lax.rem(iz + dz, gz),
        }

    def across(d):
        mirrored, step = 0, 1
        while step < gz:
            bit = lax.rem(lax.div(iz, step), 2)
            mirrored += (1 - bit if d & step else bit) * step
            step *= 2
        return mirrored

    def facing(d):
        return {"gx": ix, "gy": iy, "gz": across(d)}

    def send(src, dst, send_sem, recv_sem, target):
        copy = pltpu.make_async_remote_copy(
            src_ref=src, dst_ref=dst, send_sem=send_sem, recv_sem=recv_sem,
            device_id=target, device_id_type=MESH,
        )
        copy.start()
        return copy

    row_peers = [(a, b) for a in range(gy) for b in range(gz) if a or b]
    end_peers = [(a, b) for a in range(gx) for b in range(gz) if a or b]
    barrier = pltpu.get_barrier_semaphore()
    greeted = [peer(dy=a, dz=b) for a, b in row_peers]
    greeted += [peer(dx=a, dz=b) for a, b in end_peers if a]
    for target in greeted:
        pl.semaphore_signal(barrier, inc=1, device_id=target, device_id_type=MESH)

    my_quarter = pl.ds(pl.multiple_of(iy * quarter, 8), quarter)
    stu_stage[...] = student[my_quarter, :].astype(jnp.float32)
    for d in range(1, gz):
        first = across(d) * cols + ix * part
        tea_stage[d - 1] = teacher[pl.ds(pl.multiple_of(first, 8), part), :].astype(jnp.float32)
    pl.semaphore_wait(barrier, len(greeted))

    order = sorted(range(1, gz), key=lambda d: (bin(d).count("1"), -d))
    bits = [d for d in order if d & (d - 1) == 0]
    copies = []
    stu_first = {}
    for d in bits:
        stu_first[d] = send(
            stu_stage, stu_buf.at[d - 1, my_quarter], stu_ss.at[d - 1, 0],
            stu_rs.at[d - 1, 0], facing(d),
        )
    tea_first = {}
    for c in range(chunks):
        for d in order[::-1]:
            here = pl.ds(c * piece, piece)
            there = pl.ds(pl.multiple_of(ix * part + c * piece, 8), piece)
            tea_first[d, c] = send(
                tea_stage.at[d - 1, here], tea_buf.at[d - 1, there],
                tea_ss.at[d - 1, 0, c], tea_rs.at[d - 1, 0, c], facing(d),
            )

    def product(a, b):
        return lax.dot_general(
            a, b, (((1,), (1,)), ((), ())), preferred_element_type=jnp.float32
        )

    mine = teacher[pl.ds(pl.multiple_of(iz * cols, 8), cols), :]
    kern[...] = product(student[...], mine)

    stu_second, tea_second = {}, {}
    for d in order:
        stu_first[d].wait_recv()
        block = stu_buf.at[d - 1, my_quarter]
        for b in bits:
            if b < (d & -d):
                far = d | b
                stu_first[far] = send(
                    block, stu_buf.at[far - 1, my_quarter], stu_ss.at[far - 1, 0],
                    stu_rs.at[far - 1, 0], facing(b),
                )
        for e in range(1, gy):
            stu_second[d, e] = send(
                block, block, stu_ss.at[d - 1, e], stu_rs.at[d - 1, e], peer(dy=e)
            )
    for c in range(chunks):
        for d in order:
            tea_first[d, c].wait_recv()
            there = pl.ds(pl.multiple_of(ix * part + c * piece, 8), piece)
            block = tea_buf.at[d - 1, there]
            for e in range(1, gx):
                tea_second[d, c, e] = send(
                    block, block, tea_ss.at[d - 1, e, c], tea_rs.at[d - 1, e, c], peer(dx=e)
                )
    copies += list(stu_first.values()) + list(tea_first.values())
    copies += list(stu_second.values()) + list(tea_second.values())
    for d in order:
        for e in range(1, gy):
            stu_second[d, e].wait_recv()
        for c in range(chunks):
            for e in range(1, gx):
                tea_second[d, c, e].wait_recv()
        kern[...] += product(
            stu_buf[d - 1].astype(jnp.bfloat16), tea_buf[d - 1].astype(jnp.bfloat16)
        )

    scale = 1.0 / (math.sqrt(F) * SOFTNESS)
    first_block = (iy * gz + iz) * col_blocks
    live_slot = valid[...] > 0
    hits = [
        jnp.max(jnp.where(live_slot & (ids[...] == first_block + c), 1.0, 0.0), axis=1, keepdims=True)
        for c in range(col_blocks)
    ]

    def tile(r, c):
        return pl.ds(r * TILE, TILE), pl.ds(c * TILE, TILE)

    peaks, sums = [], []
    for r in range(row_blocks):
        on = [jnp.broadcast_to(hits[c][r : r + 1], (TILE, TILE)) > 0 for c in range(col_blocks)]
        x = [kern[tile(r, c)] * scale for c in range(col_blocks)]
        top = functools.reduce(
            jnp.maximum, [jnp.where(on[c], x[c], 0.0) for c in range(col_blocks)]
        )
        peak = jnp.maximum(jnp.max(top.T, axis=0, keepdims=True), 0.0)
        base = spread(peak)[0]
        total = jnp.zeros((TILE, TILE), jnp.float32)
        for c in range(col_blocks):
            value = jnp.where(on[c], jnp.exp(jnp.minimum(x[c] - base, 0.0)), 0.0)
            kern[tile(r, c)] = value
            total += value
        peaks.append(peak)
        sums.append(jnp.sum(total.T, axis=0, keepdims=True))
    peak = jnp.concatenate(peaks, axis=0)
    total = jnp.concatenate(sums, axis=0)

    def exchange(src, dst, send_sem, recv_sem, targets):
        for k, target in enumerate(targets):
            send(src, dst.at[k], send_sem, recv_sem, target)
        pltpu.make_async_copy(dst, dst, recv_sem).wait()

    def sent(dst, send_sem):
        pltpu.make_async_copy(dst, dst, send_sem).wait()

    row_targets = [peer(dy=a, dz=b) for a, b in row_peers]
    col_targets = [peer(dx=a) for a in range(1, gx)]
    end_targets = [peer(dx=a, dz=b) for a, b in end_peers]

    first_send[0] = peak
    first_send[1] = total
    exchange(first_send, first_recv, row_ss.at[0], row_rs.at[0], row_targets)
    highest = functools.reduce(
        jnp.maximum, [first_recv[k, 0] for k in range(len(row_peers))], peak
    )
    totals = total * jnp.exp(peak - highest)
    for k in range(len(row_peers)):
        totals += first_recv[k, 1] * jnp.exp(first_recv[k, 0] - highest)
    level = highest + jnp.log(totals + jnp.exp(-highest))
    share = jnp.exp(peak - level)
    rest = jnp.exp(-level)
    row_total = None

    for t in range(ITERS):
        if t > 0:
            weights = 1.0 / (1.0 + col_total)
            parts = []
            for r in range(row_blocks):
                total = jnp.zeros((TILE, TILE), jnp.float32)
                for c in range(col_blocks):
                    total += kern[tile(r, c)] * weights[c : c + 1]
                parts.append(jnp.sum(total.T, axis=0, keepdims=True))
            own = jnp.concatenate(parts, axis=0) * share
            row_send[t - 1] = own
            exchange(
                row_send.at[t - 1], row_recv.at[t - 1], row_ss.at[t], row_rs.at[t], row_targets
            )
            row_total = rest + own
            for k in range(len(row_peers)):
                row_total += row_recv[t - 1, k]
            factors = spread(share / row_total)
        else:
            factors = spread(share)
        parts = []
        for c in range(col_blocks):
            total = jnp.zeros((TILE, TILE), jnp.float32)
            for r in range(row_blocks):
                total += kern[tile(r, c)] * factors[r]
            parts.append(jnp.sum(total, axis=0, keepdims=True))
        own = jnp.concatenate(parts, axis=0)
        col_send[t] = own
        if t < ITERS - 1:
            exchange(col_send.at[t], col_recv.at[t], col_ss.at[t], col_rs.at[t], col_targets)
            col_total = own
            for k in range(gx - 1):
                col_total += col_recv[t, k]
        else:
            exchange(col_send.at[t], fin_recv, col_ss.at[t], col_rs.at[t], end_targets)
            for b in range(gz):
                col_total = own if b == 0 else jnp.zeros_like(own)
                for k, (_, db) in enumerate(end_peers):
                    if db == b:
                        col_total += fin_recv[k]
                col_out[lax.rem(iz + gz - b, gz)] = -SOFTNESS * jnp.log(1.0 + col_total)
    row_out[...] = -SOFTNESS * (level + jnp.log(row_total))

    for copy in copies:
        copy.wait_send()
    sent(first_recv, row_ss.at[0])
    for t in range(1, ITERS):
        sent(row_recv.at[t - 1], row_ss.at[t])
        sent(col_recv.at[t - 1], col_ss.at[t - 1])
    sent(fin_recv, col_ss.at[ITERS - 1])


def solution(mesh):
    gx, gy, gz = (mesh.shape[axis] for axis in ("gx", "gy", "gz"))
    assert gz & (gz - 1) == 0

    def on_device(student, teacher, block_ids, block_valid):
        rows, width = student.shape
        cols = teacher.shape[0] // gz
        row_blocks, col_blocks = rows // TILE, cols // TILE
        part = cols // gx
        chunks = max(1, min(4, part // 64))
        row_peers, end_peers = gy * gz - 1, gx * gz - 1
        f32 = jnp.float32
        dma = pltpu.SemaphoreType.DMA
        row, col = pl.pallas_call(
            functools.partial(kernel, (gx, gy, gz, chunks)),
            out_shape=(
                jax.ShapeDtypeStruct((row_blocks, TILE), f32),
                jax.ShapeDtypeStruct((gz, col_blocks, TILE), f32),
            ),
            in_specs=[pl.BlockSpec(memory_space=pltpu.VMEM)] * 4,
            out_specs=(pl.BlockSpec(memory_space=pltpu.VMEM),) * 2,
            scratch_shapes=[
                pltpu.VMEM((rows // gy, width), f32),
                pltpu.VMEM((gz - 1, rows, width), f32),
                pltpu.VMEM((gz - 1, part, width), f32),
                pltpu.VMEM((gz - 1, cols, width), f32),
                pltpu.VMEM((rows, cols), f32),
                pltpu.VMEM((2, row_blocks, TILE), f32),
                pltpu.VMEM((row_peers, 2, row_blocks, TILE), f32),
                pltpu.VMEM((ITERS - 1, row_blocks, TILE), f32),
                pltpu.VMEM((ITERS - 1, row_peers, row_blocks, TILE), f32),
                pltpu.VMEM((ITERS, col_blocks, TILE), f32),
                pltpu.VMEM((ITERS - 1, gx - 1, col_blocks, TILE), f32),
                pltpu.VMEM((end_peers, col_blocks, TILE), f32),
                dma((gz - 1, gy)),
                dma((gz - 1, gy)),
                dma((gz - 1, gx, chunks)),
                dma((gz - 1, gx, chunks)),
                dma((ITERS,)),
                dma((ITERS,)),
                dma((ITERS,)),
                dma((ITERS,)),
            ],
            compiler_params=pltpu.CompilerParams(collective_id=0, has_side_effects=True),
        )(student, teacher, block_ids, block_valid)
        return row.reshape(-1), col.reshape(-1)

    placed = (P("gx", "gz"), P("gy", "gz"), P("gx", None), P("gx", None))
    return jax.shard_map(
        on_device, mesh=mesh, in_specs=placed, out_specs=(P("gx"), P("gy")), check_vma=False
    )
```

```python
import functools
import math

import jax
import jax.numpy as jnp
from jax import lax
from jax.experimental import pallas as pl
from jax.experimental.pallas import tpu as pltpu
from jax.sharding import PartitionSpec as P

F = 1024
TILE = 128
ITERS = 5
SOFTNESS = 0.1
MESH = pl.DeviceIdType.MESH


def spread(values):
    return [
        jnp.broadcast_to(values[k : k + 1], (TILE, TILE)).T for k in range(values.shape[0])
    ]


def kernel(
    sizes, student, teacher, ids, valid, row_out, col_out,
    stu_stage, stu_buf, tea_stage, tea_buf, kern,
    first_send, first_recv, row_send, row_recv, col_send, col_recv, fin_recv,
    stu_ss, stu_rs, tea_ss, tea_rs, row_ss, row_rs, col_ss, col_rs,
):
    gx, gy, gz, chunks = sizes
    ix, iy, iz = lax.axis_index("gx"), lax.axis_index("gy"), lax.axis_index("gz")
    rows = student.shape[0]
    cols = teacher.shape[0] // gz
    row_blocks, col_blocks = rows // TILE, cols // TILE
    quarter = rows // gy
    part = cols // gx
    piece = part // chunks

    def peer(dx=0, dy=0, dz=0):
        return {
            "gx": lax.rem(ix + dx, gx),
            "gy": lax.rem(iy + dy, gy),
            "gz": lax.rem(iz + dz, gz),
        }

    def across(d):
        mirrored, step = 0, 1
        while step < gz:
            bit = lax.rem(lax.div(iz, step), 2)
            mirrored += (1 - bit if d & step else bit) * step
            step *= 2
        return mirrored

    def facing(d):
        return {"gx": ix, "gy": iy, "gz": across(d)}

    def send(src, dst, send_sem, recv_sem, target):
        copy = pltpu.make_async_remote_copy(
            src_ref=src, dst_ref=dst, send_sem=send_sem, recv_sem=recv_sem,
            device_id=target, device_id_type=MESH,
        )
        copy.start()
        return copy

    row_peers = [(a, b) for a in range(gy) for b in range(gz) if a or b]
    end_peers = [(a, b) for a in range(gx) for b in range(gz) if a or b]
    barrier = pltpu.get_barrier_semaphore()
    greeted = [peer(dy=a, dz=b) for a, b in row_peers]
    greeted += [peer(dx=a, dz=b) for a, b in end_peers if a]
    for target in greeted:
        pl.semaphore_signal(barrier, inc=1, device_id=target, device_id_type=MESH)

    my_quarter = pl.ds(pl.multiple_of(iy * quarter, 8), quarter)
    stu_stage[...] = student[my_quarter, :].astype(jnp.float32)
    for d in range(1, gz):
        first = across(d) * cols + ix * part
        tea_stage[d - 1] = teacher[pl.ds(pl.multiple_of(first, 8), part), :].astype(jnp.float32)
    pl.semaphore_wait(barrier, len(greeted))

    order = sorted(range(1, gz), key=lambda d: (bin(d).count("1"), -d))
    bits = [d for d in order if d & (d - 1) == 0]
    copies = []
    stu_first = {}
    for d in bits:
        stu_first[d] = send(
            stu_stage, stu_buf.at[d - 1, my_quarter], stu_ss.at[d - 1, 0],
            stu_rs.at[d - 1, 0], facing(d),
        )
    tea_first = {}
    for c in range((chunks + 1) // 2):
        for d in order[::-1]:
            here = pl.ds(c * piece, piece)
            there = pl.ds(pl.multiple_of(ix * part + c * piece, 8), piece)
            tea_first[d, c] = send(
                tea_stage.at[d - 1, here], tea_buf.at[d - 1, there],
                tea_ss.at[d - 1, 0, c], tea_rs.at[d - 1, 0, c], facing(d),
            )

    def product(a, b):
        return lax.dot_general(
            a, b, (((1,), (1,)), ((), ())), preferred_element_type=jnp.float32
        )

    mine = teacher[pl.ds(pl.multiple_of(iz * cols, 8), cols), :]
    kern[...] = product(student[...], mine)

    stu_second, tea_second = {}, {}
    for d in order:
        stu_first[d].wait_recv()
        block = stu_buf.at[d - 1, my_quarter]
        for b in bits:
            if b < (d & -d):
                far = d | b
                stu_first[far] = send(
                    block, stu_buf.at[far - 1, my_quarter], stu_ss.at[far - 1, 0],
                    stu_rs.at[far - 1, 0], facing(b),
                )
        for e in range(1, gy):
            stu_second[d, e] = send(
                block, block, stu_ss.at[d - 1, e], stu_rs.at[d - 1, e], peer(dy=e)
            )
    for c in range((chunks + 1) // 2, chunks):
        for d in order[::-1]:
            here = pl.ds(c * piece, piece)
            there = pl.ds(pl.multiple_of(ix * part + c * piece, 8), piece)
            tea_first[d, c] = send(
                tea_stage.at[d - 1, here], tea_buf.at[d - 1, there],
                tea_ss.at[d - 1, 0, c], tea_rs.at[d - 1, 0, c], facing(d),
            )

    for c in range(chunks):
        for d in order:
            tea_first[d, c].wait_recv()
            there = pl.ds(pl.multiple_of(ix * part + c * piece, 8), piece)
            block = tea_buf.at[d - 1, there]
            for e in range(1, gx):
                tea_second[d, c, e] = send(
                    block, block, tea_ss.at[d - 1, e, c], tea_rs.at[d - 1, e, c], peer(dx=e)
                )
    copies += list(stu_first.values()) + list(tea_first.values())
    copies += list(stu_second.values()) + list(tea_second.values())
    for d in order:
        for e in range(1, gy):
            stu_second[d, e].wait_recv()
        for c in range(chunks):
            for e in range(1, gx):
                tea_second[d, c, e].wait_recv()
        kern[...] += product(
            stu_buf[d - 1].astype(jnp.bfloat16), tea_buf[d - 1].astype(jnp.bfloat16)
        )

    scale = 1.0 / (math.sqrt(F) * SOFTNESS)
    first_block = (iy * gz + iz) * col_blocks
    live_slot = valid[...] > 0
    hits = [
        jnp.max(jnp.where(live_slot & (ids[...] == first_block + c), 1.0, 0.0), axis=1, keepdims=True)
        for c in range(col_blocks)
    ]

    def tile(r, c):
        return pl.ds(r * TILE, TILE), pl.ds(c * TILE, TILE)

    peaks, sums = [], []
    for r in range(row_blocks):
        on = [jnp.broadcast_to(hits[c][r : r + 1], (TILE, TILE)) > 0 for c in range(col_blocks)]
        x = [kern[tile(r, c)] * scale for c in range(col_blocks)]
        top = functools.reduce(
            jnp.maximum, [jnp.where(on[c], x[c], 0.0) for c in range(col_blocks)]
        )
        peak = jnp.maximum(jnp.max(top.T, axis=0, keepdims=True), 0.0)
        base = spread(peak)[0]
        total = jnp.zeros((TILE, TILE), jnp.float32)
        for c in range(col_blocks):
            value = jnp.where(on[c], jnp.exp(jnp.minimum(x[c] - base, 0.0)), 0.0)
            kern[tile(r, c)] = value
            total += value
        peaks.append(peak)
        sums.append(jnp.sum(total.T, axis=0, keepdims=True))
    peak = jnp.concatenate(peaks, axis=0)
    total = jnp.concatenate(sums, axis=0)

    def exchange(src, dst, send_sem, recv_sem, targets):
        for k, target in enumerate(targets):
            send(src, dst.at[k], send_sem, recv_sem, target)
        pltpu.make_async_copy(dst, dst, recv_sem).wait()

    def sent(dst, send_sem):
        pltpu.make_async_copy(dst, dst, send_sem).wait()

    row_targets = [peer(dy=a, dz=b) for a, b in row_peers]
    col_targets = [peer(dx=a) for a in range(1, gx)]
    end_targets = [peer(dx=a, dz=b) for a, b in end_peers]

    first_send[0] = peak
    first_send[1] = total
    exchange(first_send, first_recv, row_ss.at[0], row_rs.at[0], row_targets)
    highest = functools.reduce(
        jnp.maximum, [first_recv[k, 0] for k in range(len(row_peers))], peak
    )
    totals = total * jnp.exp(peak - highest)
    for k in range(len(row_peers)):
        totals += first_recv[k, 1] * jnp.exp(first_recv[k, 0] - highest)
    level = highest + jnp.log(totals + jnp.exp(-highest))
    share = jnp.exp(peak - level)
    rest = jnp.exp(-level)
    row_total = None

    for t in range(ITERS):
        if t > 0:
            weights = 1.0 / (1.0 + col_total)
            parts = []
            for r in range(row_blocks):
                total = jnp.zeros((TILE, TILE), jnp.float32)
                for c in range(col_blocks):
                    total += kern[tile(r, c)] * weights[c : c + 1]
                parts.append(jnp.sum(total.T, axis=0, keepdims=True))
            own = jnp.concatenate(parts, axis=0) * share
            row_send[t - 1] = own
            exchange(
                row_send.at[t - 1], row_recv.at[t - 1], row_ss.at[t], row_rs.at[t], row_targets
            )
            row_total = rest + own
            for k in range(len(row_peers)):
                row_total += row_recv[t - 1, k]
            factors = spread(share / row_total)
        else:
            factors = spread(share)
        parts = []
        for c in range(col_blocks):
            total = jnp.zeros((TILE, TILE), jnp.float32)
            for r in range(row_blocks):
                total += kern[tile(r, c)] * factors[r]
            parts.append(jnp.sum(total, axis=0, keepdims=True))
        own = jnp.concatenate(parts, axis=0)
        col_send[t] = own
        if t < ITERS - 1:
            exchange(col_send.at[t], col_recv.at[t], col_ss.at[t], col_rs.at[t], col_targets)
            col_total = own
            for k in range(gx - 1):
                col_total += col_recv[t, k]
        else:
            exchange(col_send.at[t], fin_recv, col_ss.at[t], col_rs.at[t], end_targets)
            for b in range(gz):
                col_total = own if b == 0 else jnp.zeros_like(own)
                for k, (_, db) in enumerate(end_peers):
                    if db == b:
                        col_total += fin_recv[k]
                col_out[lax.rem(iz + gz - b, gz)] = -SOFTNESS * jnp.log(1.0 + col_total)
    row_out[...] = -SOFTNESS * (level + jnp.log(row_total))

    for copy in copies:
        copy.wait_send()
    sent(first_recv, row_ss.at[0])
    for t in range(1, ITERS):
        sent(row_recv.at[t - 1], row_ss.at[t])
        sent(col_recv.at[t - 1], col_ss.at[t - 1])
    sent(fin_recv, col_ss.at[ITERS - 1])


def solution(mesh):
    gx, gy, gz = (mesh.shape[axis] for axis in ("gx", "gy", "gz"))
    assert gz & (gz - 1) == 0

    def on_device(student, teacher, block_ids, block_valid):
        rows, width = student.shape
        cols = teacher.shape[0] // gz
        row_blocks, col_blocks = rows // TILE, cols // TILE
        part = cols // gx
        chunks = max(1, min(4, part // 64))
        row_peers, end_peers = gy * gz - 1, gx * gz - 1
        f32 = jnp.float32
        dma = pltpu.SemaphoreType.DMA
        row, col = pl.pallas_call(
            functools.partial(kernel, (gx, gy, gz, chunks)),
            out_shape=(
                jax.ShapeDtypeStruct((row_blocks, TILE), f32),
                jax.ShapeDtypeStruct((gz, col_blocks, TILE), f32),
            ),
            in_specs=[pl.BlockSpec(memory_space=pltpu.VMEM)] * 4,
            out_specs=(pl.BlockSpec(memory_space=pltpu.VMEM),) * 2,
            scratch_shapes=[
                pltpu.VMEM((rows // gy, width), f32),
                pltpu.VMEM((gz - 1, rows, width), f32),
                pltpu.VMEM((gz - 1, part, width), f32),
                pltpu.VMEM((gz - 1, cols, width), f32),
                pltpu.VMEM((rows, cols), f32),
                pltpu.VMEM((2, row_blocks, TILE), f32),
                pltpu.VMEM((row_peers, 2, row_blocks, TILE), f32),
                pltpu.VMEM((ITERS - 1, row_blocks, TILE), f32),
                pltpu.VMEM((ITERS - 1, row_peers, row_blocks, TILE), f32),
                pltpu.VMEM((ITERS, col_blocks, TILE), f32),
                pltpu.VMEM((ITERS - 1, gx - 1, col_blocks, TILE), f32),
                pltpu.VMEM((end_peers, col_blocks, TILE), f32),
                dma((gz - 1, gy)),
                dma((gz - 1, gy)),
                dma((gz - 1, gx, chunks)),
                dma((gz - 1, gx, chunks)),
                dma((ITERS,)),
                dma((ITERS,)),
                dma((ITERS,)),
                dma((ITERS,)),
            ],
            compiler_params=pltpu.CompilerParams(collective_id=0, has_side_effects=True),
        )(student, teacher, block_ids, block_valid)
        return row.reshape(-1), col.reshape(-1)

    placed = (P("gx", "gz"), P("gy", "gz"), P("gx", None), P("gx", None))
    return jax.shard_map(
        on_device, mesh=mesh, in_specs=placed, out_specs=(P("gx"), P("gy")), check_vma=False
    )
```

```python
import functools
import math

import jax
import jax.numpy as jnp
from jax import lax
from jax.experimental import pallas as pl
from jax.experimental.pallas import tpu as pltpu
from jax.sharding import PartitionSpec as P

F = 1024
TILE = 128
ITERS = 5
SOFTNESS = 0.1
MESH = pl.DeviceIdType.MESH


def spread(values):
    return [
        jnp.broadcast_to(values[k : k + 1], (TILE, TILE)).T for k in range(values.shape[0])
    ]


def kernel(
    sizes, student_far, teacher_far, ids, valid, row_out, col_out,
    stu_stage, stu_buf, tea_stage, tea_buf, kern,
    first_send, first_recv, row_send, row_recv, col_send, col_recv, fin_recv,
    stu_ss, stu_rs, tea_ss, tea_rs, row_ss, row_rs, col_ss, col_rs, student, teacher, load_sem,
):
    gx, gy, gz, chunks = sizes
    ix, iy, iz = lax.axis_index("gx"), lax.axis_index("gy"), lax.axis_index("gz")
    rows = student.shape[0]
    cols = teacher.shape[0] // gz
    row_blocks, col_blocks = rows // TILE, cols // TILE
    quarter = rows // gy
    part = cols // gx
    piece = part // chunks

    def peer(dx=0, dy=0, dz=0):
        return {
            "gx": lax.rem(ix + dx, gx),
            "gy": lax.rem(iy + dy, gy),
            "gz": lax.rem(iz + dz, gz),
        }

    def across(d):
        mirrored, step = 0, 1
        while step < gz:
            bit = lax.rem(lax.div(iz, step), 2)
            mirrored += (1 - bit if d & step else bit) * step
            step *= 2
        return mirrored

    def facing(d):
        return {"gx": ix, "gy": iy, "gz": across(d)}

    def send(src, dst, send_sem, recv_sem, target):
        copy = pltpu.make_async_remote_copy(
            src_ref=src, dst_ref=dst, send_sem=send_sem, recv_sem=recv_sem,
            device_id=target, device_id_type=MESH,
        )
        copy.start()
        return copy

    row_peers = [(a, b) for a in range(gy) for b in range(gz) if a or b]
    end_peers = [(a, b) for a in range(gx) for b in range(gz) if a or b]
    barrier = pltpu.get_barrier_semaphore()
    greeted = [peer(dy=a, dz=b) for a, b in row_peers]
    greeted += [peer(dx=a, dz=b) for a, b in end_peers if a]
    for target in greeted:
        pl.semaphore_signal(barrier, inc=1, device_id=target, device_id_type=MESH)

    loads = [
        pltpu.make_async_copy(student_far, student, load_sem.at[0]),
        pltpu.make_async_copy(teacher_far, teacher, load_sem.at[1]),
    ]
    for load in loads:
        load.start()
    for load in loads:
        load.wait()
    my_quarter = pl.ds(pl.multiple_of(iy * quarter, 8), quarter)
    stu_stage[...] = student[my_quarter, :].astype(jnp.float32)
    for d in range(1, gz):
        first = across(d) * cols + ix * part
        tea_stage[d - 1] = teacher[pl.ds(pl.multiple_of(first, 8), part), :].astype(jnp.float32)
    pl.semaphore_wait(barrier, len(greeted))

    order = sorted(range(1, gz), key=lambda d: (bin(d).count("1"), -d))
    bits = [d for d in order if d & (d - 1) == 0]
    copies = []
    stu_first = {}
    for d in bits:
        stu_first[d] = send(
            stu_stage, stu_buf.at[d - 1, my_quarter], stu_ss.at[d - 1, 0],
            stu_rs.at[d - 1, 0], facing(d),
        )
    tea_first = {}
    for c in range((chunks + 1) // 2):
        for d in order[::-1]:
            here = pl.ds(c * piece, piece)
            there = pl.ds(pl.multiple_of(ix * part + c * piece, 8), piece)
            tea_first[d, c] = send(
                tea_stage.at[d - 1, here], tea_buf.at[d - 1, there],
                tea_ss.at[d - 1, 0, c], tea_rs.at[d - 1, 0, c], facing(d),
            )

    def product(a, b):
        return lax.dot_general(
            a, b, (((1,), (1,)), ((), ())), preferred_element_type=jnp.float32
        )

    mine = teacher[pl.ds(pl.multiple_of(iz * cols, 8), cols), :]
    kern[...] = product(student[...], mine)

    stu_second, tea_second = {}, {}
    for d in order:
        stu_first[d].wait_recv()
        block = stu_buf.at[d - 1, my_quarter]
        for b in bits:
            if b < (d & -d):
                far = d | b
                stu_first[far] = send(
                    block, stu_buf.at[far - 1, my_quarter], stu_ss.at[far - 1, 0],
                    stu_rs.at[far - 1, 0], facing(b),
                )
        for e in range(1, gy):
            stu_second[d, e] = send(
                block, block, stu_ss.at[d - 1, e], stu_rs.at[d - 1, e], peer(dy=e)
            )
    for c in range((chunks + 1) // 2, chunks):
        for d in order[::-1]:
            here = pl.ds(c * piece, piece)
            there = pl.ds(pl.multiple_of(ix * part + c * piece, 8), piece)
            tea_first[d, c] = send(
                tea_stage.at[d - 1, here], tea_buf.at[d - 1, there],
                tea_ss.at[d - 1, 0, c], tea_rs.at[d - 1, 0, c], facing(d),
            )

    for c in range(chunks):
        for d in order:
            tea_first[d, c].wait_recv()
            there = pl.ds(pl.multiple_of(ix * part + c * piece, 8), piece)
            block = tea_buf.at[d - 1, there]
            for e in range(1, gx):
                tea_second[d, c, e] = send(
                    block, block, tea_ss.at[d - 1, e, c], tea_rs.at[d - 1, e, c], peer(dx=e)
                )
    copies += list(stu_first.values()) + list(tea_first.values())
    copies += list(stu_second.values()) + list(tea_second.values())
    for d in order:
        for e in range(1, gy):
            stu_second[d, e].wait_recv()
        for c in range(chunks):
            for e in range(1, gx):
                tea_second[d, c, e].wait_recv()
        kern[...] += product(
            stu_buf[d - 1].astype(jnp.bfloat16), tea_buf[d - 1].astype(jnp.bfloat16)
        )

    scale = 1.0 / (math.sqrt(F) * SOFTNESS)
    first_block = (iy * gz + iz) * col_blocks
    live_slot = valid[...] > 0
    hits = [
        jnp.max(jnp.where(live_slot & (ids[...] == first_block + c), 1.0, 0.0), axis=1, keepdims=True)
        for c in range(col_blocks)
    ]

    def tile(r, c):
        return pl.ds(r * TILE, TILE), pl.ds(c * TILE, TILE)

    peaks, sums = [], []
    for r in range(row_blocks):
        on = [jnp.broadcast_to(hits[c][r : r + 1], (TILE, TILE)) > 0 for c in range(col_blocks)]
        x = [kern[tile(r, c)] * scale for c in range(col_blocks)]
        top = functools.reduce(
            jnp.maximum, [jnp.where(on[c], x[c], 0.0) for c in range(col_blocks)]
        )
        peak = jnp.maximum(jnp.max(top.T, axis=0, keepdims=True), 0.0)
        base = spread(peak)[0]
        total = jnp.zeros((TILE, TILE), jnp.float32)
        for c in range(col_blocks):
            value = jnp.where(on[c], jnp.exp(jnp.minimum(x[c] - base, 0.0)), 0.0)
            kern[tile(r, c)] = value
            total += value
        peaks.append(peak)
        sums.append(jnp.sum(total.T, axis=0, keepdims=True))
    peak = jnp.concatenate(peaks, axis=0)
    total = jnp.concatenate(sums, axis=0)

    def exchange(src, dst, send_sem, recv_sem, targets):
        for k, target in enumerate(targets):
            send(src, dst.at[k], send_sem, recv_sem, target)
        pltpu.make_async_copy(dst, dst, recv_sem).wait()

    def sent(dst, send_sem):
        pltpu.make_async_copy(dst, dst, send_sem).wait()

    row_targets = [peer(dy=a, dz=b) for a, b in row_peers]
    col_targets = [peer(dx=a) for a in range(1, gx)]
    end_targets = [peer(dx=a, dz=b) for a, b in end_peers]

    first_send[0] = peak
    first_send[1] = total
    exchange(first_send, first_recv, row_ss.at[0], row_rs.at[0], row_targets)
    highest = functools.reduce(
        jnp.maximum, [first_recv[k, 0] for k in range(len(row_peers))], peak
    )
    totals = total * jnp.exp(peak - highest)
    for k in range(len(row_peers)):
        totals += first_recv[k, 1] * jnp.exp(first_recv[k, 0] - highest)
    level = highest + jnp.log(totals + jnp.exp(-highest))
    share = jnp.exp(peak - level)
    rest = jnp.exp(-level)
    row_total = None

    for t in range(ITERS):
        if t > 0:
            weights = 1.0 / (1.0 + col_total)
            parts = []
            for r in range(row_blocks):
                total = jnp.zeros((TILE, TILE), jnp.float32)
                for c in range(col_blocks):
                    total += kern[tile(r, c)] * weights[c : c + 1]
                parts.append(jnp.sum(total.T, axis=0, keepdims=True))
            own = jnp.concatenate(parts, axis=0) * share
            row_send[t - 1] = own
            exchange(
                row_send.at[t - 1], row_recv.at[t - 1], row_ss.at[t], row_rs.at[t], row_targets
            )
            row_total = rest + own
            for k in range(len(row_peers)):
                row_total += row_recv[t - 1, k]
            factors = spread(share / row_total)
        else:
            factors = spread(share)
        parts = []
        for c in range(col_blocks):
            total = jnp.zeros((TILE, TILE), jnp.float32)
            for r in range(row_blocks):
                total += kern[tile(r, c)] * factors[r]
            parts.append(jnp.sum(total, axis=0, keepdims=True))
        own = jnp.concatenate(parts, axis=0)
        col_send[t] = own
        if t < ITERS - 1:
            exchange(col_send.at[t], col_recv.at[t], col_ss.at[t], col_rs.at[t], col_targets)
            col_total = own
            for k in range(gx - 1):
                col_total += col_recv[t, k]
        else:
            exchange(col_send.at[t], fin_recv, col_ss.at[t], col_rs.at[t], end_targets)
            for b in range(gz):
                col_total = own if b == 0 else jnp.zeros_like(own)
                for k, (_, db) in enumerate(end_peers):
                    if db == b:
                        col_total += fin_recv[k]
                col_out[lax.rem(iz + gz - b, gz)] = -SOFTNESS * jnp.log(1.0 + col_total)
    row_out[...] = -SOFTNESS * (level + jnp.log(row_total))

    for copy in copies:
        copy.wait_send()
    sent(first_recv, row_ss.at[0])
    for t in range(1, ITERS):
        sent(row_recv.at[t - 1], row_ss.at[t])
        sent(col_recv.at[t - 1], col_ss.at[t - 1])
    sent(fin_recv, col_ss.at[ITERS - 1])


def solution(mesh):
    gx, gy, gz = (mesh.shape[axis] for axis in ("gx", "gy", "gz"))
    assert gz & (gz - 1) == 0

    def on_device(student, teacher, block_ids, block_valid):
        rows, width = student.shape
        cols = teacher.shape[0] // gz
        row_blocks, col_blocks = rows // TILE, cols // TILE
        part = cols // gx
        chunks = max(1, min(4, part // 64))
        row_peers, end_peers = gy * gz - 1, gx * gz - 1
        f32 = jnp.float32
        dma = pltpu.SemaphoreType.DMA
        row, col = pl.pallas_call(
            functools.partial(kernel, (gx, gy, gz, chunks)),
            out_shape=(
                jax.ShapeDtypeStruct((row_blocks, TILE), f32),
                jax.ShapeDtypeStruct((gz, col_blocks, TILE), f32),
            ),
            in_specs=[pl.BlockSpec(memory_space=pl.ANY)] * 2
            + [pl.BlockSpec(memory_space=pltpu.VMEM)] * 2,
            out_specs=(pl.BlockSpec(memory_space=pltpu.VMEM),) * 2,
            scratch_shapes=[
                pltpu.VMEM((rows // gy, width), f32),
                pltpu.VMEM((gz - 1, rows, width), f32),
                pltpu.VMEM((gz - 1, part, width), f32),
                pltpu.VMEM((gz - 1, cols, width), f32),
                pltpu.VMEM((rows, cols), f32),
                pltpu.VMEM((2, row_blocks, TILE), f32),
                pltpu.VMEM((row_peers, 2, row_blocks, TILE), f32),
                pltpu.VMEM((ITERS - 1, row_blocks, TILE), f32),
                pltpu.VMEM((ITERS - 1, row_peers, row_blocks, TILE), f32),
                pltpu.VMEM((ITERS, col_blocks, TILE), f32),
                pltpu.VMEM((ITERS - 1, gx - 1, col_blocks, TILE), f32),
                pltpu.VMEM((end_peers, col_blocks, TILE), f32),
                dma((gz - 1, gy)),
                dma((gz - 1, gy)),
                dma((gz - 1, gx, chunks)),
                dma((gz - 1, gx, chunks)),
                dma((ITERS,)),
                dma((ITERS,)),
                dma((ITERS,)),
                dma((ITERS,)),
                pltpu.VMEM(student.shape, student.dtype),
                pltpu.VMEM(teacher.shape, teacher.dtype),
                dma((2,)),
            ],
            compiler_params=pltpu.CompilerParams(collective_id=0, has_side_effects=True),
        )(student, teacher, block_ids, block_valid)
        return row.reshape(-1), col.reshape(-1)

    placed = (P("gx", "gz"), P("gy", "gz"), P("gx", None), P("gx", None))
    return jax.shard_map(
        on_device, mesh=mesh, in_specs=placed, out_specs=(P("gx"), P("gy")), check_vma=False
    )
```
